256 devices in a mesh: blk: 64 (over y, x_hi, z), orb: 4 (over x_lo, core).
Axes of the slice: x: 4 (x_hi: 2, x_lo: 2; x = x_hi * 2 + x_lo), y: 4, z: 8, core: 2. Of those that a mesh axis runs over, the one named last changes fastest.
Arguments:
- orbitals: bfloat16 [32768, 8192], P('blk', 'orb'), may hold values from -0.62890625 to 0.62890625
- coulomb_near: bfloat16 [32768, 512], P('blk'), may hold values from -0.52734375 to 0.52734375
- coulomb_far: bfloat16 [32768, 512], P('blk'), may hold values from -0.52734375 to 0.52734375
Outputs:
- exchange: bfloat16 [32768, 8192], P('blk', 'orb')
The draws below stay inside these ranges and needn't reach their ends.
All inputs are finite; a program needn't handle non-finite values.
Results may differ from the reference program's by a relative error of at most 0.0049.
Values may be sent and summed in bfloat16 or wider, within the bound.
A program may use at most 64 MiB of HBM per device.

```python
import jax
import jax.numpy as jnp

NORB = 8192
BP = 512
NBLK = 64
POINTS = 32768
OFF_FAR = 16


def block_levels(own_key, extent, pieces, smallest, largest):
    level = 1.0
    for position, shards_of in pieces:
        draws = jax.random.uniform(jax.random.fold_in(jax.random.fold_in(own_key, 6), position), (shards_of,), jnp.float32, smallest / len(pieces), largest / len(pieces))
        level = level * jnp.repeat(jnp.exp(draws), extent[position] // shards_of).reshape((-1,) + (1,) * (len(extent) - 1 - position))
    return level


def gaussian(stream_key, dims, deviation, bound, cuts=(), kind=jnp.bfloat16):
    loudness = block_levels(stream_key, dims, cuts, -0.22, 0.18) if cuts else 1.0
    result = jax.random.normal(stream_key, dims, jnp.float32) * deviation * loudness
    return jnp.minimum(jnp.maximum(result, -bound), bound).astype(kind)


def setup_inputs(seed: int = 0) -> dict:
    seeds = jax.random.split(jax.random.key(seed), 4)
    orbitals = gaussian(seeds[0], (POINTS, NORB), (NORB ** -0.25), 0.62890625, ((0, 64), (1, 4)))
    coulomb_near = gaussian(seeds[1], (POINTS, BP), (2 * BP ** -0.5), 0.52734375, ((0, 64),))
    coulomb_far = gaussian(seeds[2], (POINTS, BP), (2 * BP ** -0.5), 0.52734375, ((0, 64),))
    return {"orbitals": orbitals, "coulomb_near": coulomb_near, "coulomb_far": coulomb_far}


def one_offset(blocks, slab, offset):
    partner_vals = jnp.roll(blocks, -offset, axis=0)
    gram = jnp.einsum("bpn,bqn->bpq", blocks.astype(jnp.float32), partner_vals.astype(jnp.float32))
    weighted = (gram * slab.astype(jnp.float32)).astype(jnp.bfloat16)
    own = jnp.einsum("bpq,bqn->bpn", weighted.astype(jnp.float32), partner_vals.astype(jnp.float32))
    part = jnp.einsum("bpq,bpn->bqn", weighted.astype(jnp.float32), blocks.astype(jnp.float32))
    return own + jnp.roll(part, offset, axis=0)


def reference(orbitals, coulomb_near, coulomb_far):
    blocks = orbitals.reshape(NBLK, BP, NORB)
    total = one_offset(blocks, coulomb_near.reshape(NBLK, BP, BP), 1)
    total = total + one_offset(blocks, coulomb_far.reshape(NBLK, BP, BP), OFF_FAR)
    return total.reshape(POINTS, NORB).astype(jnp.bfloat16)
```

```python
import jax
import jax.numpy as jnp
from jax import lax
from jax.sharding import PartitionSpec as P


def from_behind(value, axis, by):
    devices = lax.axis_size(axis)
    return lax.ppermute(value, axis, [(i, (i + by) % devices) for i in range(devices)])


def contract(left, right, dims):
    return lax.dot_general(left, right, (dims, ((), ())), preferred_element_type=jnp.float32)


def per_device(orbitals, coulomb_near, coulomb_far):
    far_offset = lax.axis_size("blk") // 4
    offsets = (far_offset, 1)
    slabs = (coulomb_far, coulomb_near)
    ahead = [from_behind(orbitals, "blk", -k) for k in offsets]
    behind = [from_behind(orbitals, "blk", k) for k in offsets]
    grams = [lax.psum(contract(orbitals, psi, ((1,), (1,))), "orb") for psi in ahead]
    weighted = [(g * v.astype(jnp.float32)).astype(jnp.bfloat16) for g, v in zip(grams, slabs)]
    arrived = [from_behind(w, "blk", k) for w, k in zip(weighted, offsets)]
    total = contract(weighted[0], ahead[0], ((1,), (0,)))
    total = total + contract(weighted[1], ahead[1], ((1,), (0,)))
    total = total + contract(arrived[0], behind[0], ((0,), (0,)))
    total = total + contract(arrived[1], behind[1], ((0,), (0,)))
    return total.astype(jnp.bfloat16)


def solution(mesh):
    return jax.shard_map(
        per_device,
        mesh=mesh,
        in_specs=(P("blk", "orb"), P("blk", None), P("blk", None)),
        out_specs=P("blk", "orb"),
        check_vma=False,
    )
```

```python
import functools

import jax
import jax.numpy as jnp
from jax import lax
from jax.experimental import pallas as pl
from jax.experimental.pallas import tpu as pltpu
from jax.sharding import PartitionSpec as P

MESH = pl.DeviceIdType.MESH
PIECES = 8
CHUNKS = 4
FAR = 16
DEPTH = 8
DOWN, UP = 0, 1


def contract(left, right, dims):
    return lax.dot_general(left, right, (dims, ((), ())), preferred_element_type=jnp.float32)


def kernel(
    blocks,
    psi_hbm,
    near_hbm,
    far_hbm,
    out_hbm,
    own,
    taken,
    slab,
    gram,
    gram_in,
    half_out,
    half_in,
    weight,
    weight_in,
    total,
    result,
    load_sem,
    store_sem,
    psi_send,
    psi_recv,
    pair_send,
    pair_recv,
):
    rows, width = own.shape
    piece, chunk, half = rows // PIECES, rows // CHUNKS, rows // 2
    b, o = lax.axis_index("blk"), lax.axis_index("orb")
    z, x_hi = b % DEPTH, (b // DEPTH) % 2
    core = o % 2
    sibling, across = (b, o + 1 - 2 * core), (b, (o + 2) % 4)
    turned = b + DEPTH - 2 * DEPTH * x_hi
    low, high = 1 - (z + DEPTH - 1) // DEPTH, (z + 1) // DEPTH
    ahead = (((b + FAR) % blocks, o), ((b + 1) % blocks, o))
    behind = (((b + blocks - FAR) % blocks, o), ((b + blocks - 1) % blocks, o))
    near_down = ((1 - low) * behind[1][0] + low * (turned + DEPTH - 1), o)
    near_up = ((1 - high) * ahead[1][0] + high * (turned - DEPTH + 1), o)

    mine = pl.ds(pl.multiple_of(core * half, half), half)
    other = pl.ds(pl.multiple_of((1 - core) * half, half), half)

    def stream(offset, way, source, s):
        target = ((behind[0], ahead[0]), (near_down, near_up))[offset][way]
        part = pl.ds(pl.multiple_of(s * piece, piece), piece)
        return pltpu.make_async_remote_copy(
            src_ref=source.at[part],
            dst_ref=taken.at[offset, way, part],
            send_sem=psi_send.at[offset, way, s],
            recv_sem=psi_recv.at[offset, way, s],
            device_id=target,
            device_id_type=MESH,
        )

    def arrival(offset, way, s):
        part = pl.ds(pl.multiple_of(s * piece, piece), piece)
        return pltpu.make_async_remote_copy(
            src_ref=psi_hbm.at[part],
            dst_ref=taken.at[offset, way, part],
            send_sem=psi_send.at[offset, way, s],
            recv_sem=psi_recv.at[offset, way, s],
            device_id=sibling,
            device_id_type=MESH,
        )

    def pair(kind, offset, j, source, target, device):
        return pltpu.make_async_remote_copy(
            src_ref=source,
            dst_ref=target,
            send_sem=pair_send.at[kind, offset, j],
            recv_sem=pair_recv.at[kind, offset, j],
            device_id=device,
            device_id_type=MESH,
        )

    def gram_to_sibling(k, j):
        return pair(0, k, j, gram.at[k, j, other], gram_in.at[k, j], sibling)

    def half_across(k, j):
        return pair(1, k, j, half_out.at[k, j], half_in.at[k, j], across)

    def weight_to_sibling(k, j):
        return pair(2, k, j, weight.at[k, j, mine], weight.at[k, j, mine], sibling)

    def weight_ahead(k, j):
        block = (1 - k) * ahead[0][0] + k * ahead[1][0]
        return pair(3, k, j, weight.at[k, j, mine], weight_in.at[k, j, mine], (block, o))

    def weight_on(k, j):
        return pair(4, k, j, weight_in.at[k, j, mine], weight_in.at[k, j, mine], sibling)

    def columns(j):
        return pl.ds(pl.multiple_of(j * chunk, chunk), chunk)

    loads = [
        pltpu.make_async_copy(psi_hbm, own, load_sem.at[0]),
        pltpu.make_async_copy(far_hbm, slab.at[0], load_sem.at[1]),
        pltpu.make_async_copy(near_hbm, slab.at[1], load_sem.at[2]),
    ]
    for load in loads:
        load.start()

    barrier = pltpu.get_barrier_semaphore()
    peers = (sibling, across, ahead[0], behind[0], ahead[1], behind[1], near_down, near_up)
    for peer in peers:
        pl.semaphore_signal(barrier, inc=1, device_id=peer, device_id_type=MESH)
    pl.semaphore_wait(barrier, len(peers))

    for s in range(PIECES):
        stream(0, DOWN, psi_hbm, s).start()
        stream(0, UP, psi_hbm, s).start()

        @pl.when(z > 0)
        def _():
            stream(1, DOWN, psi_hbm, s).start()

        @pl.when(z < DEPTH - 1)
        def _():
            stream(1, UP, psi_hbm, s).start()

    @pl.when((z == 0) & (x_hi == 1))
    def _():
        stream(1, DOWN, psi_hbm, 0).start()

    @pl.when((z == DEPTH - 1) & (x_hi == 0))
    def _():
        stream(1, UP, psi_hbm, 0).start()

    total[...] = jnp.zeros_like(total)
    for load in loads:
        load.wait()

    def turn(s):
        @pl.when((z == 0) & (x_hi == 0))
        def _():
            stream(1, DOWN, taken.at[0, DOWN], s).start()

        @pl.when((z == 0) & (x_hi == 1) & (s < PIECES - 1))
        def _():
            stream(1, DOWN, psi_hbm, s + 1).start()

        @pl.when((z == DEPTH - 1) & (x_hi == 1))
        def _():
            stream(1, UP, taken.at[0, UP], s).start()

        @pl.when((z == DEPTH - 1) & (x_hi == 0) & (s < PIECES - 1))
        def _():
            stream(1, UP, psi_hbm, s + 1).start()

    def weigh(k, j):
        half_across(k, j).wait_recv()
        whole = gram[k, j, mine, :] + half_in[k, j].astype(jnp.float32)
        scaled = whole * slab[k, mine, columns(j)].astype(jnp.float32)
        weight[k, j, mine, :] = scaled.astype(jnp.bfloat16)
        weight_ahead(k, j).start()
        weight_to_sibling(k, j).start()

    def add_own(k, j):
        weight_to_sibling(k, j).wait_recv()
        for n in range(4):
            part = pl.ds(n * (width // 4), width // 4)
            total[:, part] += contract(
                weight[k, j], taken[k, DOWN, columns(j), part], ((1,), (0,))
            )

    def step(i, carry):
        j, k = i // 2, i % 2
        for h in range(PIECES // CHUNKS):
            s = j * (PIECES // CHUNKS) + h
            arrival(k, DOWN, s).wait_recv()

            @pl.when(k == 0)
            def _():
                arrival(0, UP, s).wait_recv()
                turn(s)

        gram[k, j] = contract(own[...], taken[k, DOWN, columns(j), :], ((1,), (1,)))
        gram_to_sibling(k, j).start()

        @pl.when(i >= 1)
        def _():
            weigh((i + 1) % 2, (i + 1) // 2 - 1)

        gram_to_sibling(k, j).wait_recv()
        mine_now = gram[k, j, mine, :] + gram_in[k, j]
        gram[k, j, mine, :] = mine_now
        half_out[k, j] = mine_now.astype(jnp.bfloat16)
        half_across(k, j).start()

        @pl.when(i >= 2)
        def _():
            add_own(k, j - 1)

        return carry

    lax.fori_loop(0, 2 * CHUNKS, step, 0)
    weigh(1, CHUNKS - 1)

    def last_own(k, carry):
        add_own(k, CHUNKS - 1)
        return carry

    lax.fori_loop(0, 2, last_own, 0)

    def pass_on(i, carry):
        weight_ahead(i % 2, i // 2).wait_recv()
        weight_on(i % 2, i // 2).start()
        return carry

    def finish(j, carry):
        def partner(k, inner):
            weight_on(k, j).wait_recv()
            for n in range(4):
                part = pl.ds(n * (width // 4), width // 4)
                total[columns(j), part] += contract(
                    weight_in[k, j], taken[k, UP, :, part], ((0,), (0,))
                )
            return inner

        lax.fori_loop(0, 2, partner, 0)
        result[columns(j), :] = total[columns(j), :].astype(jnp.bfloat16)
        pltpu.make_async_copy(
            result.at[columns(j)], out_hbm.at[columns(j)], store_sem.at[j]
        ).start()
        return carry

    lax.fori_loop(0, 2 * CHUNKS - 2, pass_on, 0)
    for s in range(PIECES):
        arrival(1, UP, s).wait_recv()
    lax.fori_loop(0, CHUNKS - 2, finish, 0)
    lax.fori_loop(2 * CHUNKS - 2, 2 * CHUNKS, pass_on, 0)
    lax.fori_loop(CHUNKS - 2, CHUNKS, finish, 0)

    for offset in range(2):
        for way in (DOWN, UP):
            for s in range(PIECES):
                stream(offset, way, psi_hbm, s).wait_send()

    def drain(i, carry):
        k, j = i % 2, i // 2
        for sent in (gram_to_sibling, half_across, weight_to_sibling, weight_ahead, weight_on):
            sent(k, j).wait_send()
        return carry

    lax.fori_loop(0, 2 * CHUNKS, drain, 0)
    for j in range(CHUNKS):
        pltpu.make_async_copy(
            result.at[columns(j)], out_hbm.at[columns(j)], store_sem.at[j]
        ).wait()


def solution(mesh):
    blocks = mesh.shape["blk"]

    def per_device(orbitals, coulomb_near, coulomb_far):
        rows, width = orbitals.shape
        chunk, half = rows // CHUNKS, rows // 2
        chunked = (2, CHUNKS)
        return pl.pallas_call(
            functools.partial(kernel, blocks),
            out_shape=jax.ShapeDtypeStruct((rows, width), jnp.bfloat16),
            in_specs=[pl.BlockSpec(memory_space=pl.ANY)] * 3,
            out_specs=pl.BlockSpec(memory_space=pl.ANY),
            scratch_shapes=[
                pltpu.VMEM((rows, width), jnp.bfloat16),
                pltpu.VMEM((2, 2, rows, width), jnp.bfloat16),
                pltpu.VMEM((2, rows, rows), jnp.bfloat16),
                pltpu.VMEM((*chunked, rows, chunk), jnp.float32),
                pltpu.VMEM((*chunked, half, chunk), jnp.float32),
                pltpu.VMEM((*chunked, half, chunk), jnp.bfloat16),
                pltpu.VMEM((*chunked, half, chunk), jnp.bfloat16),
                pltpu.VMEM((*chunked, rows, chunk), jnp.bfloat16),
                pltpu.VMEM((*chunked, rows, chunk), jnp.bfloat16),
                pltpu.VMEM((rows, width), jnp.float32),
                pltpu.VMEM((rows, width), jnp.bfloat16),
                pltpu.SemaphoreType.DMA((3,)),
                pltpu.SemaphoreType.DMA((CHUNKS,)),
                pltpu.SemaphoreType.DMA((2, 2, PIECES)),
                pltpu.SemaphoreType.DMA((2, 2, PIECES)),
                pltpu.SemaphoreType.DMA((5, *chunked)),
                pltpu.SemaphoreType.DMA((5, *chunked)),
            ],
            compiler_params=pltpu.CompilerParams(
                collective_id=0, has_side_effects=True, vmem_limit_bytes=48 << 20
            ),
        )(orbitals, coulomb_near, coulomb_far)

    return jax.shard_map(
        per_device,
        mesh=mesh,
        in_specs=(P("blk", "orb"), P("blk", None), P("blk", None)),
        out_specs=P("blk", "orb"),
        check_vma=False,
    )
```

```python
import functools

import jax
import jax.numpy as jnp
from jax import lax
from jax.experimental import pallas as pl
from jax.experimental.pallas import tpu as pltpu
from jax.sharding import PartitionSpec as P

MESH = pl.DeviceIdType.MESH
PIECES = 16
LEAD = 2
STRAIGHT = 2
CHUNKS = 4
FAR = 16
DEPTH = 8
DOWN, UP = 0, 1


def contract(left, right, dims):
    return lax.dot_general(left, right, (dims, ((), ())), preferred_element_type=jnp.float32)


def kernel(
    blocks,
    psi_hbm,
    near_hbm,
    far_hbm,
    out_hbm,
    own,
    taken,
    slab,
    gram,
    gram_in,
    half_out,
    half_in,
    weight,
    weight_in,
    total,
    result,
    load_sem,
    store_sem,
    psi_send,
    psi_recv,
    pair_send,
    pair_recv,
):
    rows, width = own.shape
    piece, chunk, half = rows // PIECES, rows // CHUNKS, rows // 2
    b, o = lax.axis_index("blk"), lax.axis_index("orb")
    z, x_hi = b % DEPTH, (b // DEPTH) % 2
    core = o % 2
    sibling, across = (b, o + 1 - 2 * core), (b, (o + 2) % 4)
    turned = b + DEPTH - 2 * DEPTH * x_hi
    low, high = 1 - (z + DEPTH - 1) // DEPTH, (z + 1) // DEPTH
    ahead = (((b + FAR) % blocks, o), ((b + 1) % blocks, o))
    behind = (((b + blocks - FAR) % blocks, o), ((b + blocks - 1) % blocks, o))
    near_down = ((1 - low) * behind[1][0] + low * (turned + DEPTH - 1), o)
    near_up = ((1 - high) * ahead[1][0] + high * (turned - DEPTH + 1), o)

    mine = pl.ds(pl.multiple_of(core * half, half), half)
    other = pl.ds(pl.multiple_of((1 - core) * half, half), half)

    def stream(offset, way, source, s):
        straight = isinstance(s, int) and s >= PIECES - STRAIGHT
        near = (behind[1], ahead[1]) if straight else (near_down, near_up)
        target = ((behind[0], ahead[0]), near)[offset][way]
        part = pl.ds(pl.multiple_of(s * piece, piece), piece)
        return pltpu.make_async_remote_copy(
            src_ref=source.at[part],
            dst_ref=taken.at[offset, way, part],
            send_sem=psi_send.at[offset, way, s],
            recv_sem=psi_recv.at[offset, way, s],
            device_id=target,
            device_id_type=MESH,
        )

    def arrival(offset, way, s):
        part = pl.ds(pl.multiple_of(s * piece, piece), piece)
        return pltpu.make_async_remote_copy(
            src_ref=psi_hbm.at[part],
            dst_ref=taken.at[offset, way, part],
            send_sem=psi_send.at[offset, way, s],
            recv_sem=psi_recv.at[offset, way, s],
            device_id=sibling,
            device_id_type=MESH,
        )

    def pair(kind, offset, j, source, target, device):
        return pltpu.make_async_remote_copy(
            src_ref=source,
            dst_ref=target,
            send_sem=pair_send.at[kind, offset, j],
            recv_sem=pair_recv.at[kind, offset, j],
            device_id=device,
            device_id_type=MESH,
        )

    def gram_to_sibling(k, j):
        return pair(0, k, j, gram.at[k, j, other], gram_in.at[k, j], sibling)

    def half_across(k, j):
        return pair(1, k, j, half_out.at[k, j], half_in.at[k, j], across)

    def weight_to_sibling(k, j):
        return pair(2, k, j, weight.at[k, j, mine], weight.at[k, j, mine], sibling)

    def weight_ahead(k, j):
        block = (1 - k) * ahead[0][0] + k * ahead[1][0]
        return pair(3, k, j, weight.at[k, j, mine], weight_in.at[k, j, mine], (block, o))

    def weight_on(k, j):
        return pair(4, k, j, weight_in.at[k, j, mine], weight_in.at[k, j, mine], sibling)

    def columns(j):
        return pl.ds(pl.multiple_of(j * chunk, chunk), chunk)

    loads = [
        pltpu.make_async_copy(psi_hbm, own, load_sem.at[0]),
        pltpu.make_async_copy(far_hbm, slab.at[0], load_sem.at[1]),
        pltpu.make_async_copy(near_hbm, slab.at[1], load_sem.at[2]),
    ]
    for load in loads:
        load.start()

    barrier = pltpu.get_barrier_semaphore()
    peers = (sibling, across, ahead[0], behind[0], ahead[1], behind[1], near_down, near_up)
    for peer in peers:
        pl.semaphore_signal(barrier, inc=1, device_id=peer, device_id_type=MESH)
    pl.semaphore_wait(barrier, len(peers))

    for s in range(PIECES - STRAIGHT, PIECES):

        @pl.when((z == 0) & (x_hi == 0))
        def _():
            stream(1, DOWN, psi_hbm, s).start()

        @pl.when((z == DEPTH - 1) & (x_hi == 1))
        def _():
            stream(1, UP, psi_hbm, s).start()

    for s in range(PIECES):
        stream(0, DOWN, psi_hbm, s).start()
        stream(0, UP, psi_hbm, s).start()

        @pl.when((z > 0) | (x_hi == 1))
        def _():
            stream(1, DOWN, psi_hbm, s).start()

        @pl.when((z < DEPTH - 1) | (x_hi == 0))
        def _():
            stream(1, UP, psi_hbm, s).start()

    total[...] = jnp.zeros_like(total)
    for load in loads:
        load.wait()

    def forward_up(s):
        arrival(0, UP, s).wait_recv()
        stream(1, UP, taken.at[0, UP], s).start()

    def weigh(k, j):
        half_across(k, j).wait_recv()
        whole = gram[k, j, mine, :] + half_in[k, j].astype(jnp.float32)
        scaled = whole * slab[k, mine, columns(j)].astype(jnp.float32)
        weight[k, j, mine, :] = scaled.astype(jnp.bfloat16)
        weight_ahead(k, j).start()
        weight_to_sibling(k, j).start()

    def add_own(k, j):
        weight_to_sibling(k, j - 1).wait_recv()
        weight_to_sibling(k, j).wait_recv()
        left = jnp.concatenate([weight[k, j - 1], weight[k, j]], axis=1)
        span = pl.ds(pl.multiple_of((j - 1) * chunk, chunk), 2 * chunk)
        for n in range(4):
            part = pl.ds(n * (width // 4), width // 4)
            total[:, part] += contract(left, taken[k, DOWN, span, part], ((1,), (0,)))

    per = PIECES // CHUNKS
    ends = low + high

    def event(i):
        return i % 2, i // 2

    def step(i, carry):
        k, j = event(i)

        @pl.when((k == 0) & (high * x_hi == 1))
        def _():
            @pl.when(j == 0)
            def _():
                for s in range(LEAD):
                    forward_up(s)

            for h in range(per):

                @pl.when(j * per + LEAD + h < PIECES - STRAIGHT)
                def _():
                    forward_up(j * per + LEAD + h)

        for h in range(per):
            s = j * per + h
            arrival(k, DOWN, s).wait_recv()

            @pl.when((k == 0) & (low * (1 - x_hi) == 1) & (s < PIECES - STRAIGHT))
            def _():
                stream(1, DOWN, taken.at[0, DOWN], s).start()

        gram[k, j] = contract(own[...], taken[k, DOWN, columns(j), :], ((1,), (1,)))
        gram_to_sibling(k, j).start()

        @pl.when((i >= 1) & (ends == 0))
        def _():
            weigh(*event(i - 1))

        gram_to_sibling(k, j).wait_recv()
        mine_now = gram[k, j, mine, :] + gram_in[k, j]
        gram[k, j, mine, :] = mine_now
        half_out[k, j] = mine_now.astype(jnp.bfloat16)
        half_across(k, j).start()

        @pl.when((i >= 2) & (event(i - 2)[1] % 2 == 1) & (ends == 0))
        def _():
            add_own(*event(i - 2))

        return carry

    lax.fori_loop(0, 2 * CHUNKS, step, 0)
    def close(i, carry):
        @pl.when(i < 2 * CHUNKS)
        def _():
            weigh(*event(i))

        @pl.when((i >= 1) & (event(i - 1)[1] % 2 == 1))
        def _():
            add_own(*event(i - 1))

        return carry

    lax.fori_loop((1 - ends) * (2 * CHUNKS - 1), 2 * CHUNKS + 1, close, 0)

    def pass_on(i, carry):
        weight_ahead(i % 2, i // 2).wait_recv()
        weight_on(i % 2, i // 2).start()
        return carry

    def block_rows(m):
        return pl.ds(pl.multiple_of(m * 2 * chunk, 2 * chunk), 2 * chunk)

    def store(m):
        return pltpu.make_async_copy(
            result.at[block_rows(m)], out_hbm.at[block_rows(m)], store_sem.at[m]
        )

    def finish(m, carry):
        lefts = []
        for k in range(2):
            weight_on(k, 2 * m).wait_recv()
            weight_on(k, 2 * m + 1).wait_recv()
            lefts.append(jnp.concatenate([weight_in[k, 2 * m], weight_in[k, 2 * m + 1]], axis=1))
        for n in range(4):
            part = pl.ds(n * (width // 4), width // 4)
            value = total[block_rows(m), part]
            for k in range(2):
                value += contract(lefts[k], taken[k, UP, :, part], ((0,), (0,)))
            result[block_rows(m), part] = value.astype(jnp.bfloat16)
        store(m).start()
        return carry

    lax.fori_loop(0, 2 * CHUNKS - 2, pass_on, 0)
    for s in range(PIECES):
        arrival(1, UP, s).wait_recv()
        if s < PIECES - STRAIGHT:

            @pl.when(high * x_hi == 0)
            def _():
                arrival(0, UP, s).wait_recv()

        else:
            arrival(0, UP, s).wait_recv()
    lax.fori_loop(0, CHUNKS // 2 - 1, finish, 0)
    lax.fori_loop(2 * CHUNKS - 2, 2 * CHUNKS, pass_on, 0)
    lax.fori_loop(CHUNKS // 2 - 1, CHUNKS // 2, finish, 0)

    for offset in range(2):
        for way in (DOWN, UP):
            for s in range(PIECES):
                stream(offset, way, psi_hbm, s).wait_send()

    def drain(i, carry):
        k, j = i % 2, i // 2
        for sent in (gram_to_sibling, half_across, weight_to_sibling, weight_ahead, weight_on):
            sent(k, j).wait_send()
        return carry

    lax.fori_loop(0, 2 * CHUNKS, drain, 0)
    for m in range(CHUNKS // 2):
        store(m).wait()


def solution(mesh):
    blocks = mesh.shape["blk"]

    def per_device(orbitals, coulomb_near, coulomb_far):
        rows, width = orbitals.shape
        chunk, half = rows // CHUNKS, rows // 2
        chunked = (2, CHUNKS)
        return pl.pallas_call(
            functools.partial(kernel, blocks),
            out_shape=jax.ShapeDtypeStruct((rows, width), jnp.bfloat16),
            in_specs=[pl.BlockSpec(memory_space=pl.ANY)] * 3,
            out_specs=pl.BlockSpec(memory_space=pl.ANY),
            scratch_shapes=[
                pltpu.VMEM((rows, width), jnp.bfloat16),
                pltpu.VMEM((2, 2, rows, width), jnp.bfloat16),
                pltpu.VMEM((2, rows, rows), jnp.bfloat16),
                pltpu.VMEM((*chunked, rows, chunk), jnp.float32),
                pltpu.VMEM((*chunked, half, chunk), jnp.float32),
                pltpu.VMEM((*chunked, half, chunk), jnp.bfloat16),
                pltpu.VMEM((*chunked, half, chunk), jnp.bfloat16),
                pltpu.VMEM((*chunked, rows, chunk), jnp.bfloat16),
                pltpu.VMEM((*chunked, rows, chunk), jnp.bfloat16),
                pltpu.VMEM((rows, width), jnp.float32),
                pltpu.VMEM((rows, width), jnp.bfloat16),
                pltpu.SemaphoreType.DMA((3,)),
                pltpu.SemaphoreType.DMA((CHUNKS // 2,)),
                pltpu.SemaphoreType.DMA((2, 2, PIECES)),
                pltpu.SemaphoreType.DMA((2, 2, PIECES)),
                pltpu.SemaphoreType.DMA((5, *chunked)),
                pltpu.SemaphoreType.DMA((5, *chunked)),
            ],
            compiler_params=pltpu.CompilerParams(
                collective_id=0, has_side_effects=True, vmem_limit_bytes=67043328
            ),
        )(orbitals, coulomb_near, coulomb_far)

    return jax.shard_map(
        per_device,
        mesh=mesh,
        in_specs=(P("blk", "orb"), P("blk", None), P("blk", None)),
        out_specs=P("blk", "orb"),
        check_vma=False,
    )
```

```python
import functools

import jax
import jax.numpy as jnp
from jax import lax
from jax.experimental import pallas as pl
from jax.experimental.pallas import tpu as pltpu
from jax.sharding import PartitionSpec as P

MESH = pl.DeviceIdType.MESH
PIECES = 16
LEAD = 2
STRAIGHT = 2
CHUNKS = 4
FAR = 16
DEPTH = 8
DOWN, UP = 0, 1


def contract(left, right, dims):
    return lax.dot_general(left, right, (dims, ((), ())), preferred_element_type=jnp.float32)


def kernel(
    blocks,
    psi_hbm,
    near_hbm,
    far_hbm,
    out_ref,
    own,
    taken,
    slab,
    gram,
    gram_in,
    half_out,
    half_in,
    weight,
    weight_in,
    total,
    load_sem,
    psi_send,
    psi_recv,
    pair_send,
    pair_recv,
):
    rows, width = own.shape
    piece, chunk, half = rows // PIECES, rows // CHUNKS, rows // 2
    b, o = lax.axis_index("blk"), lax.axis_index("orb")
    z, x_hi = b % DEPTH, (b // DEPTH) % 2
    core = o % 2
    sibling, across = (b, o + 1 - 2 * core), (b, (o + 2) % 4)
    turned = b + DEPTH - 2 * DEPTH * x_hi
    low, high = 1 - (z + DEPTH - 1) // DEPTH, (z + 1) // DEPTH
    ahead = (((b + FAR) % blocks, o), ((b + 1) % blocks, o))
    behind = (((b + blocks - FAR) % blocks, o), ((b + blocks - 1) % blocks, o))
    near_down = ((1 - low) * behind[1][0] + low * (turned + DEPTH - 1), o)
    near_up = ((1 - high) * ahead[1][0] + high * (turned - DEPTH + 1), o)

    mine = pl.ds(pl.multiple_of(core * half, half), half)
    other = pl.ds(pl.multiple_of((1 - core) * half, half), half)

    def stream(offset, way, source, s):
        straight = isinstance(s, int) and s >= PIECES - STRAIGHT
        near = (behind[1], ahead[1]) if straight else (near_down, near_up)
        target = ((behind[0], ahead[0]), near)[offset][way]
        part = pl.ds(pl.multiple_of(s * piece, piece), piece)
        return pltpu.make_async_remote_copy(
            src_ref=source.at[part],
            dst_ref=taken.at[offset, way, part],
            send_sem=psi_send.at[offset, way, s],
            recv_sem=psi_recv.at[offset, way, s],
            device_id=target,
            device_id_type=MESH,
        )

    def arrival(offset, way, s):
        part = pl.ds(pl.multiple_of(s * piece, piece), piece)
        return pltpu.make_async_remote_copy(
            src_ref=psi_hbm.at[part],
            dst_ref=taken.at[offset, way, part],
            send_sem=psi_send.at[offset, way, s],
            recv_sem=psi_recv.at[offset, way, s],
            device_id=sibling,
            device_id_type=MESH,
        )

    def pair(kind, offset, j, source, target, device):
        return pltpu.make_async_remote_copy(
            src_ref=source,
            dst_ref=target,
            send_sem=pair_send.at[kind, offset, j],
            recv_sem=pair_recv.at[kind, offset, j],
            device_id=device,
            device_id_type=MESH,
        )

    def gram_to_sibling(k, j):
        return pair(0, k, j, gram.at[k, j, other], gram_in.at[k, j], sibling)

    def half_across(k, j):
        return pair(1, k, j, half_out.at[k, j], half_in.at[k, j], across)

    def weight_to_sibling(k, j):
        return pair(2, k, j, weight.at[k, j, mine], weight.at[k, j, mine], sibling)

    def weight_ahead(k, j):
        block = (1 - k) * ahead[0][0] + k * ahead[1][0]
        return pair(3, k, j, weight.at[k, j, mine], weight_in.at[k, j, mine], (block, o))

    def weight_on(k, j):
        return pair(4, k, j, weight_in.at[k, j, mine], weight_in.at[k, j, mine], sibling)

    def columns(j):
        return pl.ds(pl.multiple_of(j * chunk, chunk), chunk)

    loads = [
        pltpu.make_async_copy(psi_hbm, own, load_sem.at[0]),
        pltpu.make_async_copy(far_hbm, slab.at[0], load_sem.at[1]),
        pltpu.make_async_copy(near_hbm, slab.at[1], load_sem.at[2]),
    ]
    for load in loads:
        load.start()

    barrier = pltpu.get_barrier_semaphore()
    peers = (sibling, across, ahead[0], behind[0], ahead[1], behind[1], near_down, near_up)
    for peer in peers:
        pl.semaphore_signal(barrier, inc=1, device_id=peer, device_id_type=MESH)
    pl.semaphore_wait(barrier, len(peers))

    for s in range(PIECES - STRAIGHT, PIECES):

        @pl.when((z == 0) & (x_hi == 0))
        def _():
            stream(1, DOWN, psi_hbm, s).start()

        @pl.when((z == DEPTH - 1) & (x_hi == 1))
        def _():
            stream(1, UP, psi_hbm, s).start()

    for s in range(PIECES):
        stream(0, DOWN, psi_hbm, s).start()
        stream(0, UP, psi_hbm, s).start()

        @pl.when((z > 0) | (x_hi == 1))
        def _():
            stream(1, DOWN, psi_hbm, s).start()

        @pl.when((z < DEPTH - 1) | (x_hi == 0))
        def _():
            stream(1, UP, psi_hbm, s).start()

    total[...] = jnp.zeros_like(total)
    for load in loads:
        load.wait()

    def forward_up(s):
        arrival(0, UP, s).wait_recv()
        stream(1, UP, taken.at[0, UP], s).start()

    def weigh(k, j):
        half_across(k, j).wait_recv()
        whole = gram[k, j, mine, :] + half_in[k, j].astype(jnp.float32)
        scaled = whole * slab[k, mine, columns(j)].astype(jnp.float32)
        weight[k, j, mine, :] = scaled.astype(jnp.bfloat16)
        weight_ahead(k, j).start()
        weight_to_sibling(k, j).start()

    def add_own(k, j):
        weight_to_sibling(k, j - 1).wait_recv()
        weight_to_sibling(k, j).wait_recv()
        left = jnp.concatenate([weight[k, j - 1], weight[k, j]], axis=1)
        span = pl.ds(pl.multiple_of((j - 1) * chunk, chunk), 2 * chunk)
        for n in range(4):
            part = pl.ds(n * (width // 4), width // 4)
            total[:, part] += contract(left, taken[k, DOWN, span, part], ((1,), (0,)))

    per = PIECES // CHUNKS
    ends = low + high

    def event(i):
        return i % 2, i // 2

    def step(i, carry):
        k, j = event(i)

        @pl.when((k == 0) & (high * x_hi == 1))
        def _():
            @pl.when(j == 0)
            def _():
                for s in range(LEAD):
                    forward_up(s)

            for h in range(per):

                @pl.when(j * per + LEAD + h < PIECES - STRAIGHT)
                def _():
                    forward_up(j * per + LEAD + h)

        for h in range(per):
            s = j * per + h
            arrival(k, DOWN, s).wait_recv()

            @pl.when((k == 0) & (low * (1 - x_hi) == 1) & (s < PIECES - STRAIGHT))
            def _():
                stream(1, DOWN, taken.at[0, DOWN], s).start()

        gram[k, j] = contract(own[...], taken[k, DOWN, columns(j), :], ((1,), (1,)))
        gram_to_sibling(k, j).start()

        @pl.when((i >= 1) & (ends == 0))
        def _():
            weigh(*event(i - 1))

        gram_to_sibling(k, j).wait_recv()
        mine_now = gram[k, j, mine, :] + gram_in[k, j]
        gram[k, j, mine, :] = mine_now
        half_out[k, j] = mine_now.astype(jnp.bfloat16)
        half_across(k, j).start()

        @pl.when((i >= 2) & (event(i - 2)[1] % 2 == 1) & (ends == 0))
        def _():
            add_own(*event(i - 2))

        return carry

    lax.fori_loop(0, 2 * CHUNKS, step, 0)
    def close(i, carry):
        @pl.when(i < 2 * CHUNKS)
        def _():
            weigh(*event(i))

        @pl.when((i >= 1) & (event(i - 1)[1] % 2 == 1))
        def _():
            add_own(*event(i - 1))

        return carry

    lax.fori_loop((1 - ends) * (2 * CHUNKS - 1), 2 * CHUNKS + 1, close, 0)

    def pass_on(i, carry):
        weight_ahead(i % 2, i // 2).wait_recv()
        weight_on(i % 2, i // 2).start()
        return carry

    def block_rows(m):
        return pl.ds(pl.multiple_of(m * 2 * chunk, 2 * chunk), 2 * chunk)

    def finish(m, carry):
        lefts = []
        for k in range(2):
            weight_on(k, 2 * m).wait_recv()
            weight_on(k, 2 * m + 1).wait_recv()
            lefts.append(jnp.concatenate([weight_in[k, 2 * m], weight_in[k, 2 * m + 1]], axis=1))
        for n in range(4):
            part = pl.ds(n * (width // 4), width // 4)
            value = total[block_rows(m), part]
            for k in range(2):
                value += contract(lefts[k], taken[k, UP, :, part], ((0,), (0,)))
            out_ref[block_rows(m), part] = value.astype(jnp.bfloat16)
        return carry

    lax.fori_loop(0, 2 * CHUNKS - 2, pass_on, 0)
    for s in range(PIECES):
        arrival(1, UP, s).wait_recv()
        if s < PIECES - STRAIGHT:

            @pl.when(high * x_hi == 0)
            def _():
                arrival(0, UP, s).wait_recv()

        else:
            arrival(0, UP, s).wait_recv()
    lax.fori_loop(0, CHUNKS // 2 - 1, finish, 0)
    lax.fori_loop(2 * CHUNKS - 2, 2 * CHUNKS, pass_on, 0)
    lax.fori_loop(CHUNKS // 2 - 1, CHUNKS // 2, finish, 0)

    for offset in range(2):
        for way in (DOWN, UP):
            for s in range(PIECES):
                stream(offset, way, psi_hbm, s).wait_send()

    def drain(i, carry):
        k, j = i % 2, i // 2
        for sent in (gram_to_sibling, half_across, weight_to_sibling, weight_ahead, weight_on):
            sent(k, j).wait_send()
        return carry

    lax.fori_loop(0, 2 * CHUNKS, drain, 0)


def solution(mesh):
    blocks = mesh.shape["blk"]

    def per_device(orbitals, coulomb_near, coulomb_far):
        rows, width = orbitals.shape
        chunk, half = rows // CHUNKS, rows // 2
        chunked = (2, CHUNKS)
        return pl.pallas_call(
            functools.partial(kernel, blocks),
            out_shape=jax.ShapeDtypeStruct((rows, width), jnp.bfloat16),
            in_specs=[pl.BlockSpec(memory_space=pl.ANY)] * 3,
            out_specs=pl.BlockSpec(memory_space=pltpu.VMEM),
            scratch_shapes=[
                pltpu.VMEM((rows, width), jnp.bfloat16),
                pltpu.VMEM((2, 2, rows, width), jnp.bfloat16),
                pltpu.VMEM((2, rows, rows), jnp.bfloat16),
                pltpu.VMEM((*chunked, rows, chunk), jnp.float32),
                pltpu.VMEM((*chunked, half, chunk), jnp.float32),
                pltpu.VMEM((*chunked, half, chunk), jnp.bfloat16),
                pltpu.VMEM((*chunked, half, chunk), jnp.bfloat16),
                pltpu.VMEM((*chunked, rows, chunk), jnp.bfloat16),
                pltpu.VMEM((*chunked, rows, chunk), jnp.bfloat16),
                pltpu.VMEM((rows, width), jnp.float32),
                pltpu.SemaphoreType.DMA((3,)),
                pltpu.SemaphoreType.DMA((2, 2, PIECES)),
                pltpu.SemaphoreType.DMA((2, 2, PIECES)),
                pltpu.SemaphoreType.DMA((5, *chunked)),
                pltpu.SemaphoreType.DMA((5, *chunked)),
            ],
            compiler_params=pltpu.CompilerParams(
                collective_id=0, has_side_effects=True, vmem_limit_bytes=48 << 20
            ),
        )(*[pltpu.with_memory_space_constraint(v, pltpu.HBM) for v in (orbitals, coulomb_near, coulomb_far)])

    return jax.shard_map(
        per_device,
        mesh=mesh,
        in_specs=(P("blk", "orb"), P("blk", None), P("blk", None)),
        out_specs=P("blk", "orb"),
        check_vma=False,
    )
```

```python
import functools

import jax
import jax.numpy as jnp
from jax import lax
from jax.experimental import pallas as pl
from jax.experimental.pallas import tpu as pltpu
from jax.sharding import PartitionSpec as P

MESH = pl.DeviceIdType.MESH
PIECES = 16
LEAD = 2
STRAIGHT = (0, 2)
CHUNKS = 4
FAR = 16
DEPTH = 8
DOWN, UP = 0, 1


def contract(left, right, dims):
    return lax.dot_general(left, right, (dims, ((), ())), preferred_element_type=jnp.float32)


def kernel(
    blocks,
    psi_hbm,
    near_hbm,
    far_hbm,
    out_ref,
    own,
    taken,
    slab,
    gram,
    gram_in,
    half_out,
    half_in,
    weight,
    weight_in,
    total,
    load_sem,
    psi_send,
    psi_recv,
    pair_send,
    pair_recv,
    ready,
):
    rows, width = own.shape
    piece, chunk, half = rows // PIECES, rows // CHUNKS, rows // 2
    b, o = lax.axis_index("blk"), lax.axis_index("orb")
    z, x_hi = b % DEPTH, (b // DEPTH) % 2
    core = o % 2
    sibling, across = (b, o + 1 - 2 * core), (b, (o + 2) % 4)
    turned = b + DEPTH - 2 * DEPTH * x_hi
    low, high = 1 - (z + DEPTH - 1) // DEPTH, (z + 1) // DEPTH
    ahead = (((b + FAR) % blocks, o), ((b + 1) % blocks, o))
    behind = (((b + blocks - FAR) % blocks, o), ((b + blocks - 1) % blocks, o))
    near_down = ((1 - low) * behind[1][0] + low * (turned + DEPTH - 1), o)
    near_up = ((1 - high) * ahead[1][0] + high * (turned - DEPTH + 1), o)

    mine = pl.ds(pl.multiple_of(core * half, half), half)
    other = pl.ds(pl.multiple_of((1 - core) * half, half), half)

    def stream(offset, way, source, s):
        straight = isinstance(s, int) and s >= PIECES - STRAIGHT[way]
        near = (behind[1], ahead[1]) if straight else (near_down, near_up)
        target = ((behind[0], ahead[0]), near)[offset][way]
        part = pl.ds(pl.multiple_of(s * piece, piece), piece)
        return pltpu.make_async_remote_copy(
            src_ref=source.at[part],
            dst_ref=taken.at[offset, way, part],
            send_sem=psi_send.at[offset, way, s],
            recv_sem=psi_recv.at[offset, way, s],
            device_id=target,
            device_id_type=MESH,
        )

    def arrival(offset, way, s):
        part = pl.ds(pl.multiple_of(s * piece, piece), piece)
        return pltpu.make_async_remote_copy(
            src_ref=psi_hbm.at[part],
            dst_ref=taken.at[offset, way, part],
            send_sem=psi_send.at[offset, way, s],
            recv_sem=psi_recv.at[offset, way, s],
            device_id=sibling,
            device_id_type=MESH,
        )

    def pair(kind, offset, j, source, target, device):
        return pltpu.make_async_remote_copy(
            src_ref=source,
            dst_ref=target,
            send_sem=pair_send.at[kind, offset, j],
            recv_sem=pair_recv.at[kind, offset, j],
            device_id=device,
            device_id_type=MESH,
        )

    def gram_to_sibling(k, j):
        return pair(0, k, j, gram.at[k, j, other], gram_in.at[k, j], sibling)

    def half_across(k, j):
        return pair(1, k, j, half_out.at[k, j], half_in.at[k, j], across)

    def weight_to_sibling(k, j):
        return pair(2, k, j, weight.at[k, j, mine], weight.at[k, j, mine], sibling)

    def weight_ahead(k, j):
        block = (1 - k) * ahead[0][0] + k * ahead[1][0]
        return pair(3, k, j, weight.at[k, j, mine], weight_in.at[k, j, mine], (block, o))

    def weight_on(k, j):
        return pair(4, k, j, weight_in.at[k, j, mine], weight_in.at[k, j, mine], sibling)

    def columns(j):
        return pl.ds(pl.multiple_of(j * chunk, chunk), chunk)

    loads = [
        pltpu.make_async_copy(psi_hbm, own, load_sem.at[0]),
        pltpu.make_async_copy(far_hbm, slab.at[0], load_sem.at[1]),
        pltpu.make_async_copy(near_hbm, slab.at[1], load_sem.at[2]),
    ]
    for load in loads:
        load.start()

    barrier = pltpu.get_barrier_semaphore()
    for peer in (sibling, across, ahead[0], behind[0], near_down, behind[1]):
        pl.semaphore_signal(barrier, inc=1, device_id=peer, device_id_type=MESH)

    @pl.when(z < DEPTH - 1)
    def _():
        for peer in (near_up, ahead[1]):
            pl.semaphore_signal(barrier, inc=1, device_id=peer, device_id_type=MESH)

    @pl.when(z == 0)
    def _():
        pl.semaphore_wait(barrier, 6)

    @pl.when(z > 0)
    def _():
        pl.semaphore_wait(barrier, 8)

    @pl.when(z == DEPTH - 1)
    def _():
        for peer in (near_up, ahead[1]):
            pl.semaphore_signal(ready, inc=1, device_id=peer, device_id_type=MESH)

    for s in range(PIECES - STRAIGHT[UP], PIECES):

        @pl.when((z == DEPTH - 1) & (x_hi == 1))
        def _():
            stream(1, UP, psi_hbm, s).start()

    for s in range(PIECES):
        stream(0, DOWN, psi_hbm, s).start()
        stream(0, UP, psi_hbm, s).start()

        @pl.when(z > 0)
        def _():
            stream(1, DOWN, psi_hbm, s).start()

        @pl.when((z < DEPTH - 1) | (x_hi == 0))
        def _():
            stream(1, UP, psi_hbm, s).start()

    @pl.when(z == 0)
    def _():
        pl.semaphore_wait(ready, 2)
        for s in range(PIECES - STRAIGHT[DOWN], PIECES):

            @pl.when(x_hi == 0)
            def _():
                stream(1, DOWN, psi_hbm, s).start()

        for s in range(PIECES):

            @pl.when(x_hi == 1)
            def _():
                stream(1, DOWN, psi_hbm, s).start()

    total[...] = jnp.zeros_like(total)
    for load in loads:
        load.wait()

    def forward_up(s):
        arrival(0, UP, s).wait_recv()
        stream(1, UP, taken.at[0, UP], s).start()

    def weigh(k, j):
        half_across(k, j).wait_recv()
        whole = gram[k, j, mine, :] + half_in[k, j].astype(jnp.float32)
        scaled = whole * slab[k, mine, columns(j)].astype(jnp.float32)
        weight[k, j, mine, :] = scaled.astype(jnp.bfloat16)
        weight_ahead(k, j).start()
        weight_to_sibling(k, j).start()

    def add_own(k, j):
        weight_to_sibling(k, j - 1).wait_recv()
        weight_to_sibling(k, j).wait_recv()
        left = jnp.concatenate([weight[k, j - 1], weight[k, j]], axis=1)
        span = pl.ds(pl.multiple_of((j - 1) * chunk, chunk), 2 * chunk)
        for n in range(4):
            part = pl.ds(n * (width // 4), width // 4)
            total[:, part] += contract(left, taken[k, DOWN, span, part], ((1,), (0,)))

    per = PIECES // CHUNKS
    ends = low + high

    def event(i):
        late = i // (2 * CHUNKS - 4) * ends
        k = (1 - late) * (i % 2) + late * (i % 4 // 2)
        j = (1 - late) * (i // 2) + late * (CHUNKS - 2 + i % 2)
        return (k + high) % 2, j

    def step(i, carry):
        k, j = event(i)

        @pl.when((i % 2 == 0) & (high * x_hi == 1))
        def _():
            @pl.when(i == 0)
            def _():
                for s in range(LEAD):
                    forward_up(s)

            for h in range(per):

                @pl.when(i // 2 * per + LEAD + h < PIECES - STRAIGHT[UP])
                def _():
                    forward_up(i // 2 * per + LEAD + h)

        for h in range(per):
            s = j * per + h
            arrival(k, DOWN, s).wait_recv()

            @pl.when((k == 0) & (low * (1 - x_hi) == 1) & (s < PIECES - STRAIGHT[DOWN]))
            def _():
                stream(1, DOWN, taken.at[0, DOWN], s).start()

        gram[k, j] = contract(own[...], taken[k, DOWN, columns(j), :], ((1,), (1,)))
        gram_to_sibling(k, j).start()

        @pl.when((i >= 1) & (ends == 0))
        def _():
            weigh(*event(i - 1))

        gram_to_sibling(k, j).wait_recv()
        mine_now = gram[k, j, mine, :] + gram_in[k, j]
        gram[k, j, mine, :] = mine_now
        half_out[k, j] = mine_now.astype(jnp.bfloat16)
        half_across(k, j).start()

        @pl.when((i >= 2) & (event(i - 2)[1] % 2 == 1) & (ends == 0))
        def _():
            add_own(*event(i - 2))

        return carry

    lax.fori_loop(0, 2 * CHUNKS, step, 0)
    def close(i, carry):
        @pl.when(i < 2 * CHUNKS)
        def _():
            weigh(*event(i))

        @pl.when((i >= 1) & (event(i - 1)[1] % 2 == 1) & (ends == 0))
        def _():
            add_own(*event(i - 1))

        return carry

    lax.fori_loop((1 - ends) * (2 * CHUNKS - 1), 2 * CHUNKS + 1, close, 0)

    @pl.when(ends == 1)
    def _():
        def own_last(i, carry):
            add_own(i % 2, i // 2 * 2 + 1)
            return carry

        lax.fori_loop(0, CHUNKS, own_last, 0)

    def pass_on(i, carry):
        weight_ahead(i % 2, i // 2).wait_recv()
        weight_on(i % 2, i // 2).start()
        return carry

    def block_rows(m):
        return pl.ds(pl.multiple_of(m * 2 * chunk, 2 * chunk), 2 * chunk)

    def finish(m, carry):
        lefts = []
        for k in range(2):
            weight_on(k, 2 * m).wait_recv()
            weight_on(k, 2 * m + 1).wait_recv()
            lefts.append(jnp.concatenate([weight_in[k, 2 * m], weight_in[k, 2 * m + 1]], axis=1))
        for n in range(4):
            part = pl.ds(n * (width // 4), width // 4)
            value = total[block_rows(m), part]
            for k in range(2):
                value += contract(lefts[k], taken[k, UP, :, part], ((0,), (0,)))
            out_ref[block_rows(m), part] = value.astype(jnp.bfloat16)
        return carry

    lax.fori_loop(0, 2 * CHUNKS - 2, pass_on, 0)
    for s in range(PIECES):
        arrival(1, UP, s).wait_recv()
        if s < PIECES - STRAIGHT[UP]:

            @pl.when(high * x_hi == 0)
            def _():
                arrival(0, UP, s).wait_recv()

        else:
            arrival(0, UP, s).wait_recv()
    lax.fori_loop(0, CHUNKS // 2 - 1, finish, 0)
    lax.fori_loop(2 * CHUNKS - 2, 2 * CHUNKS, pass_on, 0)
    lax.fori_loop(CHUNKS // 2 - 1, CHUNKS // 2, finish, 0)

    for offset in range(2):
        for way in (DOWN, UP):
            for s in range(PIECES):
                stream(offset, way, psi_hbm, s).wait_send()

    def drain(i, carry):
        k, j = i % 2, i // 2
        for sent in (gram_to_sibling, half_across, weight_to_sibling, weight_ahead, weight_on):
            sent(k, j).wait_send()
        return carry

    lax.fori_loop(0, 2 * CHUNKS, drain, 0)


def solution(mesh):
    blocks = mesh.shape["blk"]

    def per_device(orbitals, coulomb_near, coulomb_far):
        rows, width = orbitals.shape
        chunk, half = rows // CHUNKS, rows // 2
        chunked = (2, CHUNKS)
        return pl.pallas_call(
            functools.partial(kernel, blocks),
            out_shape=jax.ShapeDtypeStruct((rows, width), jnp.bfloat16),
            in_specs=[pl.BlockSpec(memory_space=pl.ANY)] * 3,
            out_specs=pl.BlockSpec(memory_space=pltpu.VMEM),
            scratch_shapes=[
                pltpu.VMEM((rows, width), jnp.bfloat16),
                pltpu.VMEM((2, 2, rows, width), jnp.bfloat16),
                pltpu.VMEM((2, rows, rows), jnp.bfloat16),
                pltpu.VMEM((*chunked, rows, chunk), jnp.float32),
                pltpu.VMEM((*chunked, half, chunk), jnp.float32),
                pltpu.VMEM((*chunked, half, chunk), jnp.bfloat16),
                pltpu.VMEM((*chunked, half, chunk), jnp.bfloat16),
                pltpu.VMEM((*chunked, rows, chunk), jnp.bfloat16),
                pltpu.VMEM((*chunked, rows, chunk), jnp.bfloat16),
                pltpu.VMEM((rows, width), jnp.float32),
                pltpu.SemaphoreType.DMA((3,)),
                pltpu.SemaphoreType.DMA((2, 2, PIECES)),
                pltpu.SemaphoreType.DMA((2, 2, PIECES)),
                pltpu.SemaphoreType.DMA((5, *chunked)),
                pltpu.SemaphoreType.DMA((5, *chunked)),
                pltpu.SemaphoreType.REGULAR,
            ],
            compiler_params=pltpu.CompilerParams(
                collective_id=0, has_side_effects=True, vmem_limit_bytes=48 << 20
            ),
        )(*[pltpu.with_memory_space_constraint(v, pltpu.HBM) for v in (orbitals, coulomb_near, coulomb_far)])

    return jax.shard_map(
        per_device,
        mesh=mesh,
        in_specs=(P("blk", "orb"), P("blk", None), P("blk", None)),
        out_specs=P("blk", "orb"),
        check_vma=False,
    )
```

```python
import functools

import jax
import jax.numpy as jnp
from jax import lax
from jax.experimental import pallas as pl
from jax.experimental.pallas import tpu as pltpu
from jax.sharding import PartitionSpec as P

MESH = pl.DeviceIdType.MESH
PIECES = 16
LEAD = 2
STRAIGHT = (0, 1)
CHUNKS = 4
FAR = 16
DEPTH = 8
DOWN, UP = 0, 1


def contract(left, right, dims):
    return lax.dot_general(left, right, (dims, ((), ())), preferred_element_type=jnp.float32)


def kernel(
    blocks,
    psi_hbm,
    near_hbm,
    far_hbm,
    out_ref,
    own,
    taken,
    slab,
    gram,
    gram_in,
    half_out,
    half_in,
    weight,
    weight_in,
    total,
    load_sem,
    psi_send,
    psi_recv,
    pair_send,
    pair_recv,
    ready,
):
    rows, width = own.shape
    piece, chunk, half = rows // PIECES, rows // CHUNKS, rows // 2
    b, o = lax.axis_index("blk"), lax.axis_index("orb")
    z, x_hi = b % DEPTH, (b // DEPTH) % 2
    core = o % 2
    sibling, across = (b, o + 1 - 2 * core), (b, (o + 2) % 4)
    turned = b + DEPTH - 2 * DEPTH * x_hi
    low, high = 1 - (z + DEPTH - 1) // DEPTH, (z + 1) // DEPTH
    ahead = (((b + FAR) % blocks, o), ((b + 1) % blocks, o))
    behind = (((b + blocks - FAR) % blocks, o), ((b + blocks - 1) % blocks, o))
    near_down = ((1 - low) * behind[1][0] + low * (turned + DEPTH - 1), o)
    near_up = ((1 - high) * ahead[1][0] + high * (turned - DEPTH + 1), o)

    mine = pl.ds(pl.multiple_of(core * half, half), half)
    other = pl.ds(pl.multiple_of((1 - core) * half, half), half)

    def stream(offset, way, source, s):
        straight = isinstance(s, int) and s >= PIECES - STRAIGHT[way]
        near = (behind[1], ahead[1]) if straight else (near_down, near_up)
        target = ((behind[0], ahead[0]), near)[offset][way]
        part = pl.ds(pl.multiple_of(s * piece, piece), piece)
        return pltpu.make_async_remote_copy(
            src_ref=source.at[part],
            dst_ref=taken.at[offset, way, part],
            send_sem=psi_send.at[offset, way, s],
            recv_sem=psi_recv.at[offset, way, s],
            device_id=target,
            device_id_type=MESH,
        )

    def arrival(offset, way, s):
        part = pl.ds(pl.multiple_of(s * piece, piece), piece)
        return pltpu.make_async_remote_copy(
            src_ref=psi_hbm.at[part],
            dst_ref=taken.at[offset, way, part],
            send_sem=psi_send.at[offset, way, s],
            recv_sem=psi_recv.at[offset, way, s],
            device_id=sibling,
            device_id_type=MESH,
        )

    def pair(kind, offset, j, source, target, device):
        return pltpu.make_async_remote_copy(
            src_ref=source,
            dst_ref=target,
            send_sem=pair_send.at[kind, offset, j],
            recv_sem=pair_recv.at[kind, offset, j],
            device_id=device,
            device_id_type=MESH,
        )

    def gram_to_sibling(k, j):
        return pair(0, k, j, gram.at[k, j, other], gram_in.at[k, j], sibling)

    def half_across(k, j):
        return pair(1, k, j, half_out.at[k, j], half_in.at[k, j], across)

    def weight_to_sibling(k, j):
        return pair(2, k, j, weight.at[k, j, mine], weight.at[k, j, mine], sibling)

    def weight_ahead(k, j):
        block = (1 - k) * ahead[0][0] + k * ahead[1][0]
        return pair(3, k, j, weight.at[k, j, mine], weight_in.at[k, j, mine], (block, o))

    def weight_on(k, j):
        return pair(4, k, j, weight_in.at[k, j, mine], weight_in.at[k, j, mine], sibling)

    def columns(j):
        return pl.ds(pl.multiple_of(j * chunk, chunk), chunk)

    loads = [
        pltpu.make_async_copy(psi_hbm, own, load_sem.at[0]),
        pltpu.make_async_copy(far_hbm, slab.at[0], load_sem.at[1]),
        pltpu.make_async_copy(near_hbm, slab.at[1], load_sem.at[2]),
    ]
    for load in loads:
        load.start()

    barrier = pltpu.get_barrier_semaphore()
    for peer in (sibling, across, ahead[0], behind[0], near_down, behind[1]):
        pl.semaphore_signal(barrier, inc=1, device_id=peer, device_id_type=MESH)

    @pl.when(z < DEPTH - 1)
    def _():
        for peer in (near_up, ahead[1]):
            pl.semaphore_signal(barrier, inc=1, device_id=peer, device_id_type=MESH)

    @pl.when(z == 0)
    def _():
        pl.semaphore_wait(barrier, 6)

    @pl.when(z > 0)
    def _():
        pl.semaphore_wait(barrier, 8)

    @pl.when(z == DEPTH - 1)
    def _():
        for peer in (near_up, ahead[1]):
            pl.semaphore_signal(ready, inc=1, device_id=peer, device_id_type=MESH)

    for s in range(PIECES - STRAIGHT[UP], PIECES):

        @pl.when((z == DEPTH - 1) & (x_hi == 1))
        def _():
            stream(1, UP, psi_hbm, s).start()

    for s in range(PIECES):
        stream(0, DOWN, psi_hbm, s).start()
        stream(0, UP, psi_hbm, s).start()

        @pl.when(z > 0)
        def _():
            stream(1, DOWN, psi_hbm, s).start()

        @pl.when((z < DEPTH - 1) | (x_hi == 0))
        def _():
            stream(1, UP, psi_hbm, s).start()

    @pl.when(z == 0)
    def _():
        pl.semaphore_wait(ready, 2)
        for s in range(PIECES - STRAIGHT[DOWN], PIECES):

            @pl.when(x_hi == 0)
            def _():
                stream(1, DOWN, psi_hbm, s).start()

        for s in range(PIECES):

            @pl.when(x_hi == 1)
            def _():
                stream(1, DOWN, psi_hbm, s).start()

    total[...] = jnp.zeros_like(total)
    for load in loads:
        load.wait()

    def forward_up(s):
        arrival(0, UP, s).wait_recv()
        stream(1, UP, taken.at[0, UP], s).start()

    def weigh(k, j):
        half_across(k, j).wait_recv()
        whole = gram[k, j, mine, :] + half_in[k, j].astype(jnp.float32)
        scaled = whole * slab[k, mine, columns(j)].astype(jnp.float32)
        weight[k, j, mine, :] = scaled.astype(jnp.bfloat16)
        weight_ahead(k, j).start()
        weight_to_sibling(k, j).start()

    def add_own(k, j):
        weight_to_sibling(k, j - 1).wait_recv()
        weight_to_sibling(k, j).wait_recv()
        left = jnp.concatenate([weight[k, j - 1], weight[k, j]], axis=1)
        span = pl.ds(pl.multiple_of((j - 1) * chunk, chunk), 2 * chunk)
        for n in range(4):
            part = pl.ds(n * (width // 4), width // 4)
            total[:, part] += contract(left, taken[k, DOWN, span, part], ((1,), (0,)))

    per = PIECES // CHUNKS
    ends = low + high

    def event(i):
        late = i // (2 * CHUNKS - 4) * ends
        k = (1 - late) * (i % 2) + late * (i % 4 // 2)
        j = (1 - late) * (i // 2) + late * (CHUNKS - 2 + i % 2)
        return (k + high) % 2, j

    def step(i, carry):
        k, j = event(i)

        @pl.when((i % 2 == 0) & (high * x_hi == 1))
        def _():
            @pl.when(i == 0)
            def _():
                for s in range(LEAD):
                    forward_up(s)

            for h in range(per):

                @pl.when(i // 2 * per + LEAD + h < PIECES - STRAIGHT[UP])
                def _():
                    forward_up(i // 2 * per + LEAD + h)

        for h in range(per):
            s = j * per + h
            arrival(k, DOWN, s).wait_recv()

            @pl.when((k == 0) & (low * (1 - x_hi) == 1) & (s < PIECES - STRAIGHT[DOWN]))
            def _():
                stream(1, DOWN, taken.at[0, DOWN], s).start()

        gram[k, j] = contract(own[...], taken[k, DOWN, columns(j), :], ((1,), (1,)))
        gram_to_sibling(k, j).start()

        @pl.when((i >= 1) & (ends == 0))
        def _():
            weigh(*event(i - 1))

        gram_to_sibling(k, j).wait_recv()
        mine_now = gram[k, j, mine, :] + gram_in[k, j]
        gram[k, j, mine, :] = mine_now
        half_out[k, j] = mine_now.astype(jnp.bfloat16)
        half_across(k, j).start()

        @pl.when((i >= 2) & (event(i - 2)[1] % 2 == 1) & (ends == 0))
        def _():
            add_own(*event(i - 2))

        return carry

    lax.fori_loop(0, 2 * CHUNKS, step, 0)
    def close(i, carry):
        @pl.when(i < 2 * CHUNKS)
        def _():
            weigh(*event(i))

        @pl.when((i >= 1) & (event(i - 1)[1] % 2 == 1) & (ends == 0))
        def _():
            add_own(*event(i - 1))

        return carry

    lax.fori_loop((1 - ends) * (2 * CHUNKS - 1), 2 * CHUNKS + 1, close, 0)

    @pl.when(ends == 1)
    def _():
        def own_last(i, carry):
            add_own(i % 2, i // 2 * 2 + 1)
            return carry

        lax.fori_loop(0, CHUNKS, own_last, 0)

    def pass_on(i, carry):
        weight_ahead(i % 2, i // 2).wait_recv()
        weight_on(i % 2, i // 2).start()
        return carry

    def block_rows(m):
        return pl.ds(pl.multiple_of(m * 2 * chunk, 2 * chunk), 2 * chunk)

    def finish(m, carry):
        lefts = []
        for k in range(2):
            weight_on(k, 2 * m).wait_recv()
            weight_on(k, 2 * m + 1).wait_recv()
            lefts.append(jnp.concatenate([weight_in[k, 2 * m], weight_in[k, 2 * m + 1]], axis=1))
        for n in range(4):
            part = pl.ds(n * (width // 4), width // 4)
            value = total[block_rows(m), part]
            for k in range(2):
                value += contract(lefts[k], taken[k, UP, :, part], ((0,), (0,)))
            out_ref[block_rows(m), part] = value.astype(jnp.bfloat16)
        return carry

    lax.fori_loop(0, 2 * CHUNKS - 2, pass_on, 0)
    for s in range(PIECES):
        arrival(1, UP, s).wait_recv()
        if s < PIECES - STRAIGHT[UP]:

            @pl.when(high * x_hi == 0)
            def _():
                arrival(0, UP, s).wait_recv()

        else:
            arrival(0, UP, s).wait_recv()
    lax.fori_loop(0, CHUNKS // 2 - 1, finish, 0)
    lax.fori_loop(2 * CHUNKS - 2, 2 * CHUNKS, pass_on, 0)
    lax.fori_loop(CHUNKS // 2 - 1, CHUNKS // 2, finish, 0)

    for offset in range(2):
        for way in (DOWN, UP):
            for s in range(PIECES):
                stream(offset, way, psi_hbm, s).wait_send()

    def drain(i, carry):
        k, j = i % 2, i // 2
        for sent in (gram_to_sibling, half_across, weight_to_sibling, weight_ahead, weight_on):
            sent(k, j).wait_send()
        return carry

    lax.fori_loop(0, 2 * CHUNKS, drain, 0)


def solution(mesh):
    blocks = mesh.shape["blk"]

    def per_device(orbitals, coulomb_near, coulomb_far):
        rows, width = orbitals.shape
        chunk, half = rows // CHUNKS, rows // 2
        chunked = (2, CHUNKS)
        return pl.pallas_call(
            functools.partial(kernel, blocks),
            out_shape=jax.ShapeDtypeStruct((rows, width), jnp.bfloat16),
            in_specs=[pl.BlockSpec(memory_space=pl.ANY)] * 3,
            out_specs=pl.BlockSpec(memory_space=pltpu.VMEM),
            scratch_shapes=[
                pltpu.VMEM((rows, width), jnp.bfloat16),
                pltpu.VMEM((2, 2, rows, width), jnp.bfloat16),
                pltpu.VMEM((2, rows, rows), jnp.bfloat16),
                pltpu.VMEM((*chunked, rows, chunk), jnp.float32),
                pltpu.VMEM((*chunked, half, chunk), jnp.float32),
                pltpu.VMEM((*chunked, half, chunk), jnp.bfloat16),
                pltpu.VMEM((*chunked, half, chunk), jnp.bfloat16),
                pltpu.VMEM((*chunked, rows, chunk), jnp.bfloat16),
                pltpu.VMEM((*chunked, rows, chunk), jnp.bfloat16),
                pltpu.VMEM((rows, width), jnp.float32),
                pltpu.SemaphoreType.DMA((3,)),
                pltpu.SemaphoreType.DMA((2, 2, PIECES)),
                pltpu.SemaphoreType.DMA((2, 2, PIECES)),
                pltpu.SemaphoreType.DMA((5, *chunked)),
                pltpu.SemaphoreType.DMA((5, *chunked)),
                pltpu.SemaphoreType.REGULAR,
            ],
            compiler_params=pltpu.CompilerParams(
                collective_id=0, has_side_effects=True, vmem_limit_bytes=48 << 20
            ),
        )(*[pltpu.with_memory_space_constraint(v, pltpu.HBM) for v in (orbitals, coulomb_near, coulomb_far)])

    return jax.shard_map(
        per_device,
        mesh=mesh,
        in_specs=(P("blk", "orb"), P("blk", None), P("blk", None)),
        out_specs=P("blk", "orb"),
        check_vma=False,
    )
```
